768 devices in a mesh: seq: 64 (over x, y, core), head: 12 (over z).
Axes of the slice: x: 4, y: 8, z: 12, core: 2. Of those that a mesh axis runs over, the one named last changes fastest.
Arguments:
- queries: bfloat16 [32768, 3072], P('seq', 'head'), may hold values from -6 to 6
- key_feats: bfloat16 [32768, 3072], P('seq', 'head'), may hold values from -6 to 6
- value_feats: bfloat16 [32768, 3072], P('seq', 'head'), may hold values from -140 to 140
- targets: bfloat16 [32768, 3072], P('seq', 'head'), may hold values from -6 to 6
- norm_gain: float32 [3072], P('head'), may hold values from 0.5 to 1.5
- doc_lengths: int32 [20], replicated, may hold values from 1 to 8192, 32768 in all
Outputs:
- normed: bfloat16 [32768, 3072], P('seq', 'head')
- grad_queries: bfloat16 [32768, 3072], P('seq', 'head')
- grad_keys: bfloat16 [32768, 3072], P('seq', 'head')
- grad_values: bfloat16 [32768, 3072], P('seq', 'head')
The draws below stay inside these ranges and needn't reach their ends.
Inputs may be any that keep to these rules, and one draw needn't show every extreme that they name: `doc_lengths`: lengths of the 20 documents packed in order into the 32768 positions; they sum to 32768 and the longest is exactly 8192.
All inputs are finite; a program needn't handle non-finite values.
Results may differ from the reference program's by a relative error of at most 0.015.
Values sent between devices are 32-bit elements; how exact they have to be, the bound alone decides.
A program may use at most 32 MiB of HBM per device.

```python
import math
import jax
import jax.numpy as jnp
import numpy as np
from jax import lax

DH = 128
TOK_DEV = 512
HEADS = 24
TOKENS = 32768
DOCS = 20
MAXDOC = 8192


def draw_value_feats(key, part):
    noise_key, row_key, col_key = jax.random.split(key, 3)
    width_all = HEADS * DH
    noise = jnp.clip(jax.random.normal(noise_key, (TOKENS, width_all), jnp.float32), -4.0, 4.0)
    growth = 3.0
    row_scale = jnp.exp(jax.random.uniform(row_key, (TOKENS, 1), jnp.float32, math.log(0.3), math.log(3.0)))
    head_place = jnp.arange(width_all, dtype=jnp.float32) // DH / max(HEADS - 1, 1)
    column_scale = 0.3 * growth ** head_place * jnp.exp(jax.random.uniform(col_key, (width_all,), jnp.float32, 0.0, math.log(10.0)))
    return (noise * row_scale * column_scale[None, :]).astype(jnp.bfloat16)


def level_of(rng, shape, shards, low, largest):
    def one(position, blocks):
        draws = jax.random.uniform(jax.random.fold_in(jax.random.fold_in(rng, 6), position), (blocks,), jnp.float32, low / len(shards), largest / len(shards))
        return jnp.repeat(jnp.exp(draws), shape[position] // blocks).reshape((-1,) + (1,) * (len(shape) - position - 1))

    gain = one(*shards[0])
    for cut in shards[1:]:
        gain = gain * one(*cut)
    return gain


def split_up(count, total, limit, skew):
    loads = [(1 << 20) // math.isqrt(grade ** skew) + 1 for grade in range(2, count + 1)]
    spare, given = total - limit - (count - 1), [1] * (count - 1)
    while spare > 0:
        movable = [i for i in range(count - 1) if given[i] < limit]
        mass, remaining = sum([loads[i] for i in movable]), spare
        for i in movable:
            extra = min(limit - given[i], max(1, remaining * loads[i] // mass), spare)
            given[i] = given[i] + extra
            spare = spare - extra
    return np.array([limit] + given)


def ragged_sizes(own_key, amount, total, reach, skew):
    if amount == 2:
        one = jax.random.randint(own_key, (), max(1, total - reach), min(reach, total - 1) + 1)
        return jnp.stack([one, total - one])
    tallies = jnp.asarray(split_up(amount, total, reach, skew), jnp.int32)
    pairs = (amount - 1) // 2
    donor, receiver = tallies[1:1 + 2 * pairs:2], tallies[2:2 + 2 * pairs:2]
    margin = jnp.minimum(donor - 1, reach - receiver)
    shifted = jax.random.randint(jax.random.fold_in(own_key, 1), (pairs,), 0, 1 << 20) % (margin + 1)
    tallies = tallies.at[1:1 + 2 * pairs:2].set(donor - shifted).at[2:2 + 2 * pairs:2].set(receiver + shifted)
    return tallies[jax.random.permutation(jax.random.fold_in(own_key, 2), amount)]


def bell_draw(own_key, extent, spread, reach, pieces=(), kind=jnp.bfloat16):
    gain = level_of(own_key, extent, pieces, -0.22, 0.18) if pieces else 1.0
    drawn = jax.random.normal(own_key, extent, jnp.float32) * spread * gain
    return jnp.minimum(jnp.maximum(drawn, -reach), reach).astype(kind)


def setup_inputs(seed: int = 0) -> dict:
    arg_keys = jax.random.split(jax.random.key(seed), 7)
    return {
        "queries": bell_draw(arg_keys[0], (TOKENS, HEADS * DH), 1.0, 6.0, ((0, 64), (1, 12))),
        "key_feats": bell_draw(arg_keys[1], (TOKENS, HEADS * DH), 1.0, 6.0, ((0, 64), (1, 12))),
        "value_feats": draw_value_feats(jax.random.fold_in(arg_keys[6], 71), 0),
        "targets": bell_draw(arg_keys[3], (TOKENS, HEADS * DH), 1.0, 6.0, ((0, 64), (1, 12))),
        "norm_gain": jnp.clip(1.0 + 0.1 * jax.random.normal(arg_keys[4], (HEADS * DH,), jnp.float32), 0.5, 1.5),
        "doc_lengths": ragged_sizes(arg_keys[5], DOCS, TOKENS, MAXDOC, 2).astype(jnp.int32),
    }


def document_ids(doc_lengths, positions):
    doc_ends = jnp.cumsum(doc_lengths, dtype=jnp.int32)
    return lax.optimization_barrier(jnp.sum((doc_ends[None, :] <= positions[:, None]).astype(jnp.int32), axis=1, dtype=jnp.int32))

def reference(queries, key_feats, value_feats, targets, norm_gain, doc_lengths):
    blocks = TOKENS // TOK_DEV
    width_all = HEADS * DH

    def split_rows(array):
        return array.reshape(blocks, TOK_DEV, HEADS, DH)
    positions = jnp.arange(TOKENS, dtype=jnp.int32)
    token_docs = document_ids(doc_lengths, positions).reshape(blocks, TOK_DEV)
    block_starts = jnp.arange(blocks, dtype=jnp.int32) * TOK_DEV
    prev_docs = document_ids(doc_lengths, block_starts - 1)
    next_docs = document_ids(doc_lengths, block_starts + TOK_DEV)
    causal = jnp.arange(TOK_DEV)[:, None] >= jnp.arange(TOK_DEV)[None, :]
    gain_three = norm_gain.reshape(1, HEADS, DH).astype(jnp.float32)

    def forward_step(carry, inputs):
        query_blk, key_blk, value_blk, target_blk, docs, prev_doc = inputs
        query_f = query_blk.astype(jnp.float32)
        key_f = key_blk.astype(jnp.float32)
        value_f = value_blk.astype(jnp.float32)
        same_doc = causal & (docs[:, None] == docs[None, :])
        use_in = (docs == prev_doc).astype(jnp.float32)[:, None, None]
        carry_low = lax.optimization_barrier(carry.astype(jnp.bfloat16))
        scores = jnp.einsum('thd,shd->hts', query_f, key_f)
        attn = lax.optimization_barrier(jnp.where(same_doc[None], scores, 0.0).astype(jnp.bfloat16))
        output = jnp.einsum('hts,she->the', attn.astype(jnp.float32), value_f)
        output = output + use_in * jnp.einsum('thd,hde->the', query_f, carry_low.astype(jnp.float32))
        square_sum = lax.optimization_barrier(jnp.sum(output * output, axis=(1, 2)))
        inverse = lax.rsqrt(square_sum / width_all + 1e-06)[:, None, None]
        normed = lax.optimization_barrier((gain_three * output * inverse).astype(jnp.bfloat16))
        grad_normed = normed.astype(jnp.float32) - target_blk.astype(jnp.float32)
        weighted = gain_three * grad_normed
        slope = lax.optimization_barrier(jnp.sum(weighted * output, axis=(1, 2)))[:, None, None]
        grad_output = weighted * inverse - output * (slope * inverse ** 3 / width_all)
        grad_output = lax.optimization_barrier(grad_output.astype(jnp.bfloat16))
        in_last = (docs == docs[-1]).astype(jnp.float32)[:, None, None]
        in_first = (docs == docs[0]).astype(jnp.float32)[:, None, None]
        local_state = jnp.einsum('thd,the->hde', key_f * in_last, value_f)
        flag = (docs[-1] != prev_doc).astype(jnp.float32)
        new_carry = local_state + (1.0 - flag) * carry
        tail_state = jnp.einsum('thd,the->hde', query_f * in_first, grad_output.astype(jnp.float32))
        return (new_carry, (normed, grad_output, carry_low, tail_state))
    start_state = jnp.zeros((HEADS, DH, DH), jnp.float32)
    forward_inputs = (split_rows(queries), split_rows(key_feats), split_rows(value_feats), split_rows(targets), token_docs, prev_docs)
    final_state, saved = lax.scan(forward_step, start_state, forward_inputs)
    normed_all, grad_output_all, carry_all, tail_all = saved

    def reverse_step(suffix, inputs):
        query_blk, key_blk, value_blk, grad_output, carry_low, tail_state, docs, prev_doc, next_doc = inputs
        query_f = query_blk.astype(jnp.float32)
        key_f = key_blk.astype(jnp.float32)
        value_f = value_blk.astype(jnp.float32)
        grad_f = grad_output.astype(jnp.float32)
        same_doc = causal & (docs[:, None] == docs[None, :])
        use_in = (docs == prev_doc).astype(jnp.float32)[:, None, None]
        use_out = (docs == next_doc).astype(jnp.float32)[:, None, None]
        suffix_low = lax.optimization_barrier(suffix.astype(jnp.bfloat16)).astype(jnp.float32)
        scores = jnp.einsum('thd,shd->hts', query_f, key_f)
        attn = lax.optimization_barrier(jnp.where(same_doc[None], scores, 0.0).astype(jnp.bfloat16)).astype(jnp.float32)
        mixing = jnp.einsum('the,she->hts', grad_f, value_f)
        mixing = lax.optimization_barrier(jnp.where(same_doc[None], mixing, 0.0).astype(jnp.bfloat16)).astype(jnp.float32)
        grad_q = jnp.einsum('hts,shd->thd', mixing, key_f) + use_in * jnp.einsum('the,hde->thd', grad_f, carry_low.astype(jnp.float32))
        grad_k = jnp.einsum('hts,thd->shd', mixing, query_f) + use_out * jnp.einsum('she,hde->shd', value_f, suffix_low)
        grad_v = jnp.einsum('hts,the->she', attn, grad_f) + use_out * jnp.einsum('shd,hde->she', key_f, suffix_low)
        flag = (docs[0] != next_doc).astype(jnp.float32)
        new_suffix = tail_state + (1.0 - flag) * suffix
        return (new_suffix, (grad_q.astype(jnp.bfloat16), grad_k.astype(jnp.bfloat16), grad_v.astype(jnp.bfloat16)))
    reverse_inputs = (split_rows(queries), split_rows(key_feats), split_rows(value_feats), grad_output_all, carry_all, tail_all, token_docs, prev_docs, next_docs)
    last_suffix, grads = lax.scan(reverse_step, start_state, reverse_inputs, reverse=True)
    grad_q_all, grad_k_all, grad_v_all = grads
    return (normed_all.reshape(TOKENS, width_all), grad_q_all.reshape(TOKENS, width_all), grad_k_all.reshape(TOKENS, width_all), grad_v_all.reshape(TOKENS, width_all))
```

```python
import functools

import jax
import jax.numpy as jnp
from jax import lax
from jax.experimental import pallas as pl
from jax.experimental.pallas import tpu as pltpu
from jax.sharding import PartitionSpec as P

DH = 128
MAXDOC = 8192
MESH = pl.DeviceIdType.MESH
F32 = jnp.float32
BF16 = jnp.bfloat16


def contract(a, b, dims):
    return lax.dot_general(a, b, (dims, ((), ())), preferred_element_type=F32)


NN = ((1,), (0,))
NT = ((1,), (1,))
TN = ((0,), (0,))


def kernel(
    seqs, ring, zs, len_ref,
    q_ref, k_ref, v_ref, t_ref, g_ref,
    normed_ref, gq_ref, gk_ref, gv_ref,
    flag_ref, loc_ref, gat_ref, tot_ref, totin_ref, car_ref, carin_ref,
    attn_ref, mix_ref, out_ref, go_ref, sums_ref, sumsin_ref,
    ssem, rsem, tsem, zsend, zrecv,
):
    tok, width = q_ref.shape
    heads = width // DH
    width_all = width * zs
    groups = seqs // ring
    docs = len_ref.shape[0]
    device = lax.axis_index("seq")
    z = lax.axis_index("head")
    place = lax.rem(device, ring)
    group = device // ring
    base = group * ring
    after = lax.rem(device + ring, seqs)
    before = lax.rem(device + seqs - ring, seqs)

    barrier = pltpu.get_barrier_semaphore()

    def greet_ring(i, carry):
        pl.semaphore_signal(
            barrier, inc=1, device_id=(base + lax.rem(place + i, ring), z), device_id_type=MESH
        )
        return carry

    def greet_heads(i, carry):
        pl.semaphore_signal(
            barrier, inc=1, device_id=(device, lax.rem(z + i, zs)), device_id_type=MESH
        )
        return carry

    lax.fori_loop(1, ring, greet_ring, 0)
    pl.semaphore_signal(barrier, inc=1, device_id=(after, z), device_id_type=MESH)
    pl.semaphore_signal(barrier, inc=1, device_id=(before, z), device_id_type=MESH)
    lax.fori_loop(1, zs, greet_heads, 0)

    ends = []
    total = jnp.int32(0)
    for d in range(docs):
        total = total + len_ref[d]
        ends.append(total)
    first = device * tok
    last = first + tok - 1
    far = jnp.int32(2**30)
    start_last = jnp.int32(0)
    start_next = jnp.int32(0)
    end_first = far
    end_prev = far
    for e in ends:
        start_last = jnp.where(e <= last, e, start_last)
        start_next = jnp.where(e <= last + 1, e, start_next)
    for e in reversed(ends):
        end_first = jnp.where(e > first, e, end_first)
        end_prev = jnp.where(e > first - 1, e, end_prev)

    def per_row(shape):
        return first + lax.broadcasted_iota(jnp.int32, shape, 0)

    row_pos = per_row((tok, DH))
    in_last = row_pos >= start_last
    in_first = row_pos < end_first
    use_in = row_pos < end_prev
    use_out = row_pos >= start_next

    def head(ref, h):
        return ref[:, h * DH : (h + 1) * DH]

    def keep(mask, x):
        return jnp.where(mask, x.astype(F32), 0.0)

    slices = heads * DH // ring

    def put_state(which, h, state):
        per_head = DH // slices
        loc_ref[which, h * per_head : (h + 1) * per_head] = state.reshape(per_head, slices, DH)

    for h in range(heads):
        put_state(0, h, contract(keep(in_last, head(k_ref, h)).astype(BF16), head(v_ref, h), TN))

    block_first = (base + lax.broadcasted_iota(jnp.int32, (ring, DH), 0)) * tok
    cut_f = jnp.zeros((ring, DH), jnp.int32)
    cut_r = jnp.zeros((ring, DH), jnp.int32)
    for e in ends:
        cut_f = cut_f | jnp.where((e >= block_first) & (e < block_first + tok), 1, 0)
        cut_r = cut_r | jnp.where((e > block_first) & (e <= block_first + tok), 1, 0)
    flag_ref[0] = 1.0 - cut_f.astype(F32)
    flag_ref[1] = 1.0 - cut_r.astype(F32)

    column_pos = first + lax.broadcasted_iota(jnp.int32, (1, tok), 1)
    end_of = jnp.full((1, tok), far, jnp.int32)
    for e in reversed(ends):
        end_of = jnp.where(e > column_pos, e, end_of)
    tall = per_row((tok, tok))
    wide = first + lax.broadcasted_iota(jnp.int32, (tok, tok), 1)
    same_doc = (tall >= wide) & (tall < end_of)

    def slice_copy(which, stage, i):
        src, dst = ((loc_ref, gat_ref), (car_ref, carin_ref))[stage]
        peer = lax.rem(place + i, ring)
        return pltpu.make_async_remote_copy(
            src_ref=src.at[which, peer],
            dst_ref=dst.at[which, place],
            send_sem=ssem.at[which, stage, i],
            recv_sem=rsem.at[which, stage, i],
            device_id=(base + peer, z),
            device_id_type=MESH,
        )

    def start_slices(which, stage):
        def one(i, carry):
            slice_copy(which, stage, i).start()
            return carry

        lax.fori_loop(1, ring, one, 0)

    def wait_slices(which, stage):
        def one(i, carry):
            slice_copy(which, stage, i).wait()
            return carry

        lax.fori_loop(1, ring, one, 0)

    def total_copy(which):
        return pltpu.make_async_remote_copy(
            src_ref=tot_ref.at[which],
            dst_ref=totin_ref.at[which],
            send_sem=tsem.at[which, 0],
            recv_sem=tsem.at[which, 1],
            device_id=(before if which else after, z),
            device_id_type=MESH,
        )

    def order(which):
        return reversed(range(ring)) if which else range(ring)

    def gather_states(which):
        gat_ref[which, place] = loc_ref[which, place]
        start_slices(which, 0)

    def fold_column(which):
        wait_slices(which, 0)
        run = jnp.zeros((slices, DH), F32)
        for j in order(which):
            run = gat_ref[which, j] + flag_ref[which, j : j + 1] * run
        tot_ref[which] = run
        total_copy(which).start()

    def hand_out(which):
        total_copy(which).wait()
        inside = group < groups - 1 if which else group > 0
        run = jnp.where(inside, totin_ref[which], 0.0)
        for j in order(which):
            car_ref[which, j] = run
            run = gat_ref[which, j] + flag_ref[which, j : j + 1] * run
        carin_ref[which, place] = car_ref[which, place]
        start_slices(which, 1)

    def take_state(which, h):
        per_head = DH // slices
        part = carin_ref[which, h * per_head : (h + 1) * per_head]
        return part.reshape(DH, DH).astype(BF16)

    def attend(h):
        scores = contract(head(q_ref, h), head(k_ref, h), NT)
        attn_ref[h] = jnp.where(same_doc, scores, 0.0).astype(BF16)

    def local_output(h):
        out_ref[:, h * DH : (h + 1) * DH] = contract(attn_ref[h], head(v_ref, h), NN)

    pl.semaphore_wait(barrier, ring + zs)
    gather_states(0)
    for h in range(heads):
        attend(h)
    for h in range(heads):
        local_output(h)
    fold_column(0)
    hand_out(0)
    wait_slices(0, 1)

    gain = g_ref[...]
    squares = jnp.zeros((tok, 1), F32)
    gained = jnp.zeros((tok, 1), F32)
    crossed = jnp.zeros((tok, 1), F32)
    for h in range(heads):
        out = head(out_ref, h) + keep(use_in, contract(head(q_ref, h), take_state(0, h), NN))
        out_ref[:, h * DH : (h + 1) * DH] = out
        scaled = gain[:, h * DH : (h + 1) * DH] * out
        squares = squares + jnp.sum(out * out, axis=1, keepdims=True)
        gained = gained + jnp.sum(scaled * scaled, axis=1, keepdims=True)
        crossed = crossed + jnp.sum(scaled * head(t_ref, h).astype(F32), axis=1, keepdims=True)
    lane = lax.broadcasted_iota(jnp.int32, (tok, DH), 1)
    packed = jnp.where(lane == 0, squares, jnp.where(lane == 1, gained, crossed))
    sums_ref[...] = packed.T[0 : sums_ref.shape[0]]
    sumsin_ref[z] = sums_ref[...]

    def sum_copy(i):
        return pltpu.make_async_remote_copy(
            src_ref=sums_ref,
            dst_ref=sumsin_ref.at[z],
            send_sem=zsend.at[i],
            recv_sem=zrecv.at[i],
            device_id=(device, lax.rem(z + i, zs)),
            device_id_type=MESH,
        )

    def start_sum(i, carry):
        sum_copy(i).start()
        return carry

    def wait_sum(i, carry):
        sum_copy(i).wait()
        return carry

    lax.fori_loop(1, zs, start_sum, 0)
    lax.fori_loop(1, zs, wait_sum, 0)
    summed = sumsin_ref[0]
    for i in range(1, zs):
        summed = summed + sumsin_ref[i]
    inverse_row = lax.rsqrt(summed[0:1] / width_all + 1e-06)
    slope_row = inverse_row * summed[1:2] - summed[2:3]
    pull_row = slope_row * (inverse_row * inverse_row * inverse_row) / width_all
    inverse = jnp.broadcast_to(inverse_row, (DH, tok)).T
    pull = jnp.broadcast_to(pull_row, (DH, tok)).T
    for h in range(heads):
        cols = slice(h * DH, (h + 1) * DH)
        out = out_ref[:, cols]
        gain_h = gain[:, cols]
        normed = (gain_h * out * inverse).astype(BF16)
        normed_ref[:, cols] = normed
        weighted = gain_h * (normed.astype(F32) - t_ref[:, cols].astype(F32))
        grad = (weighted * inverse - out * pull).astype(BF16)
        go_ref[:, cols] = grad
        put_state(1, h, contract(keep(in_first, head(q_ref, h)).astype(BF16), grad, TN))
    gather_states(1)

    def mix(h):
        mixing = contract(head(go_ref, h), head(v_ref, h), NT)
        mix_ref[h] = jnp.where(same_doc, mixing, 0.0).astype(BF16)

    def query_grad(h):
        far_part = contract(head(go_ref, h), take_state(0, h), NT)
        near = contract(mix_ref[h], head(k_ref, h), NN)
        gq_ref[:, h * DH : (h + 1) * DH] = (near + keep(use_in, far_part)).astype(BF16)

    def near_grads(h):
        return (
            contract(mix_ref[h], head(q_ref, h), TN),
            contract(attn_ref[h], head(go_ref, h), TN),
        )

    for h in range(heads):
        mix(h)
        query_grad(h)
    fold_column(1)
    hand_out(1)
    near = [near_grads(h) for h in range(heads)]
    wait_slices(1, 1)
    for h in range(heads):
        suffix = take_state(1, h)
        cols = slice(h * DH, (h + 1) * DH)
        far_k = contract(head(v_ref, h), suffix, NT)
        far_v = contract(head(k_ref, h), suffix, NN)
        gk_ref[:, cols] = (near[h][0] + keep(use_out, far_k)).astype(BF16)
        gv_ref[:, cols] = (near[h][1] + keep(use_out, far_v)).astype(BF16)


def solution(mesh):
    seqs, zs = mesh.shape["seq"], mesh.shape["head"]

    def per_device(queries, key_feats, value_feats, targets, norm_gain, doc_lengths):
        tok, width = queries.shape
        ring = MAXDOC // tok
        heads = width // DH
        slices = width // ring
        states = pltpu.VMEM((2, ring, slices, DH), F32)
        vmem = pl.BlockSpec(memory_space=pltpu.VMEM)
        return tuple(
            pl.pallas_call(
                functools.partial(kernel, seqs, ring, zs),
                out_shape=[jax.ShapeDtypeStruct((tok, width), BF16)] * 4,
                in_specs=[pl.BlockSpec(memory_space=pltpu.SMEM)] + [vmem] * 5,
                out_specs=[vmem] * 4,
                scratch_shapes=[
                    pltpu.VMEM((2, ring, DH), F32),
                    states,
                    states,
                    pltpu.VMEM((2, slices, DH), F32),
                    pltpu.VMEM((2, slices, DH), F32),
                    states,
                    states,
                    pltpu.VMEM((heads, tok, tok), BF16),
                    pltpu.VMEM((heads, tok, tok), BF16),
                    pltpu.VMEM((tok, width), F32),
                    pltpu.VMEM((tok, width), BF16),
                    pltpu.VMEM((4, tok), F32),
                    pltpu.VMEM((zs, 4, tok), F32),
                    pltpu.SemaphoreType.DMA((2, 2, ring)),
                    pltpu.SemaphoreType.DMA((2, 2, ring)),
                    pltpu.SemaphoreType.DMA((2, 2)),
                    pltpu.SemaphoreType.DMA((zs,)),
                    pltpu.SemaphoreType.DMA((zs,)),
                ],
                compiler_params=pltpu.CompilerParams(collective_id=0, has_side_effects=True),
            )(
                doc_lengths,
                queries,
                key_feats,
                value_feats,
                targets,
                norm_gain.reshape(1, width),
            )
        )

    spec = P("seq", "head")
    return jax.shard_map(
        per_device,
        mesh=mesh,
        in_specs=(spec, spec, spec, spec, P("head"), P()),
        out_specs=(spec, spec, spec, spec),
        check_vma=False,
    )
```

```python
import functools

import jax
import jax.numpy as jnp
from jax import lax
from jax.experimental import pallas as pl
from jax.experimental.pallas import tpu as pltpu
from jax.sharding import PartitionSpec as P

DH = 128
MAXDOC = 8192
MESH = pl.DeviceIdType.MESH
F32 = jnp.float32
BF16 = jnp.bfloat16


def contract(a, b, dims):
    return lax.dot_general(a, b, (dims, ((), ())), preferred_element_type=F32)


NN = ((1,), (0,))
NT = ((1,), (1,))
TN = ((0,), (0,))


def far_first(n):
    return sorted(range(1, n), key=lambda i: -min(i, n - i))


def kernel(
    seqs, ring, zs, len_in,
    q_in, k_in, v_in, t_in, g_in,
    normed_ref, gq_ref, gk_ref, gv_ref,
    len_ref, q_ref, k_ref, v_ref, t_ref, g_ref, flag_ref, loc_ref, gat_ref, tot_ref, totin_ref, car_ref, carin_ref,
    attn_ref, mix_ref, out_ref, go_ref, sums_ref, sumsin_ref,
    load_sem, ssem, rsem, tsem, zsend, zrecv,
):
    tok, width = q_ref.shape
    heads = width // DH
    rows = tok // DH
    width_all = width * zs
    groups = seqs // ring
    docs = len_ref.shape[0]
    device = lax.axis_index("seq")
    z = lax.axis_index("head")
    place = lax.rem(device, ring)
    group = device // ring
    base = group * ring
    after = lax.rem(device + ring, seqs)
    before = lax.rem(device + seqs - ring, seqs)

    barrier = pltpu.get_barrier_semaphore()

    for i in far_first(zs):
        pl.semaphore_signal(
            barrier, inc=1, device_id=(device, lax.rem(z + i, zs)), device_id_type=MESH
        )
    for i in far_first(ring):
        pl.semaphore_signal(
            barrier, inc=1, device_id=(base + lax.rem(place + i, ring), z), device_id_type=MESH
        )
    pl.semaphore_signal(barrier, inc=1, device_id=(after, z), device_id_type=MESH)
    pl.semaphore_signal(barrier, inc=1, device_id=(before, z), device_id_type=MESH)

    loads = [
        pltpu.make_async_copy(src, dst, load_sem.at[i])
        for i, (src, dst) in enumerate(
            (
                (len_in, len_ref),
                (k_in, k_ref),
                (v_in, v_ref),
                (q_in, q_ref),
                (t_in, t_ref),
                (g_in, g_ref),
            )
        )
    ]
    for load in loads:
        load.start()
    loads[0].wait()

    ends = []
    total = jnp.int32(0)
    for d in range(docs):
        total = total + len_ref[d]
        ends.append(total)
    first = device * tok
    last = first + tok - 1
    far = jnp.int32(2**30)
    start_last = jnp.int32(0)
    start_next = jnp.int32(0)
    end_first = far
    end_prev = far
    for e in ends:
        start_last = jnp.where(e <= last, e, start_last)
        start_next = jnp.where(e <= last + 1, e, start_next)
    for e in reversed(ends):
        end_first = jnp.where(e > first, e, end_first)
        end_prev = jnp.where(e > first - 1, e, end_prev)

    def per_row(shape):
        return first + lax.broadcasted_iota(jnp.int32, shape, 0)

    row_pos = per_row((tok, DH))
    in_last = row_pos >= start_last
    in_first = row_pos < end_first
    use_in = row_pos < end_prev
    use_out = row_pos >= start_next

    def head(ref, h):
        return ref[:, h * DH : (h + 1) * DH]

    def keep(mask, x):
        return jnp.where(mask, x.astype(F32), 0.0)

    slices = heads * DH // ring

    def put_state(which, h, state):
        per_head = DH // slices
        loc_ref[which, h * per_head : (h + 1) * per_head] = state.reshape(per_head, slices, DH)

    loads[1].wait()
    loads[2].wait()
    for h in range(heads):
        put_state(0, h, contract(keep(in_last, head(k_ref, h)).astype(BF16), head(v_ref, h), TN))

    block_first = (base + lax.broadcasted_iota(jnp.int32, (ring, DH), 0)) * tok
    cut_f = jnp.zeros((ring, DH), jnp.int32)
    cut_r = jnp.zeros((ring, DH), jnp.int32)
    for e in ends:
        cut_f = cut_f | jnp.where((e >= block_first) & (e < block_first + tok), 1, 0)
        cut_r = cut_r | jnp.where((e > block_first) & (e <= block_first + tok), 1, 0)
    flag_ref[0] = 1.0 - cut_f.astype(F32)
    flag_ref[1] = 1.0 - cut_r.astype(F32)

    column_pos = first + lax.broadcasted_iota(jnp.int32, (1, tok), 1)
    end_of = jnp.full((1, tok), far, jnp.int32)
    for e in reversed(ends):
        end_of = jnp.where(e > column_pos, e, end_of)
    tall = per_row((tok, tok))
    wide = first + lax.broadcasted_iota(jnp.int32, (tok, tok), 1)
    same_doc = (tall >= wide) & (tall < end_of)

    def slice_copy(which, stage, i):
        src, dst = ((loc_ref, gat_ref), (car_ref, carin_ref))[stage]
        peer = lax.rem(place + i, ring)
        return pltpu.make_async_remote_copy(
            src_ref=src.at[which, peer],
            dst_ref=dst.at[which, place],
            send_sem=ssem.at[which, stage, i],
            recv_sem=rsem.at[which, stage, i],
            device_id=(base + peer, z),
            device_id_type=MESH,
        )

    def start_slices(which, stage):
        for i in far_first(ring):
            slice_copy(which, stage, i).start()

    def wait_slices(which, stage):
        def one(i, carry):
            slice_copy(which, stage, i).wait()
            return carry

        lax.fori_loop(1, ring, one, 0)

    def total_copy(which):
        return pltpu.make_async_remote_copy(
            src_ref=tot_ref.at[which],
            dst_ref=totin_ref.at[which],
            send_sem=tsem.at[which, 0],
            recv_sem=tsem.at[which, 1],
            device_id=(before if which else after, z),
            device_id_type=MESH,
        )

    def order(which):
        return reversed(range(ring)) if which else range(ring)

    def gather_states(which):
        gat_ref[which, place] = loc_ref[which, place]
        start_slices(which, 0)

    def fold_column(which):
        wait_slices(which, 0)
        run = jnp.zeros((slices, DH), F32)
        for j in order(which):
            run = gat_ref[which, j] + flag_ref[which, j : j + 1] * run
        tot_ref[which] = run
        total_copy(which).start()

    def hand_out(which):
        total_copy(which).wait()
        inside = group < groups - 1 if which else group > 0
        run = jnp.where(inside, totin_ref[which], 0.0)
        for j in order(which):
            car_ref[which, j] = run
            run = gat_ref[which, j] + flag_ref[which, j : j + 1] * run
        carin_ref[which, place] = car_ref[which, place]
        start_slices(which, 1)

    def take_state(which, h):
        per_head = DH // slices
        part = carin_ref[which, h * per_head : (h + 1) * per_head]
        return part.reshape(DH, DH).astype(BF16)

    def attend(h):
        scores = contract(head(q_ref, h), head(k_ref, h), NT)
        attn_ref[h] = jnp.where(same_doc, scores, 0.0).astype(BF16)

    def local_output(h):
        out_ref[:, h * DH : (h + 1) * DH] = contract(attn_ref[h], head(v_ref, h), NN)

    pl.semaphore_wait(barrier, ring + zs)
    gather_states(0)
    loads[3].wait()
    loads[4].wait()
    loads[5].wait()
    for h in range(heads):
        attend(h)
    for h in range(heads):
        local_output(h)
    fold_column(0)
    hand_out(0)
    wait_slices(0, 1)

    gain = g_ref[...]
    squares = jnp.zeros((tok, DH), F32)
    gained = jnp.zeros((tok, DH), F32)
    crossed = jnp.zeros((tok, DH), F32)
    for h in range(heads):
        out = head(out_ref, h) + keep(use_in, contract(head(q_ref, h), take_state(0, h), NN))
        out_ref[:, h * DH : (h + 1) * DH] = out
        scaled = gain[:, h * DH : (h + 1) * DH] * out
        squares = squares + out * out
        gained = gained + scaled * scaled
        crossed = crossed + scaled * head(t_ref, h).astype(F32)
    lane = lax.broadcasted_iota(jnp.int32, (tok, DH), 1)
    packed = jnp.where(
        lane == 0,
        jnp.sum(squares, axis=1, keepdims=True),
        jnp.where(
            lane == 1,
            jnp.sum(gained, axis=1, keepdims=True),
            jnp.sum(crossed, axis=1, keepdims=True),
        ),
    )
    for c in range(rows):
        turned = packed[c * DH : (c + 1) * DH].T
        for r in range(3):
            sums_ref[r * rows + c : r * rows + c + 1] = turned[r : r + 1]
    sumsin_ref[z] = sums_ref[...]

    def sum_copy(i):
        return pltpu.make_async_remote_copy(
            src_ref=sums_ref,
            dst_ref=sumsin_ref.at[z],
            send_sem=zsend.at[i],
            recv_sem=zrecv.at[i],
            device_id=(device, lax.rem(z + i, zs)),
            device_id_type=MESH,
        )

    for i in far_first(zs):
        sum_copy(i).start()
    for i in range(1, zs):
        sum_copy(i).wait()
    summed = sumsin_ref[0]
    for i in range(1, zs):
        summed = summed + sumsin_ref[i]
    inverse_rows = lax.rsqrt(summed[0:rows] / width_all + 1e-06)
    slope_rows = inverse_rows * summed[rows : 2 * rows] - summed[2 * rows : 3 * rows]
    pull_rows = slope_rows * (inverse_rows * inverse_rows * inverse_rows) / width_all

    def upright(x):
        return jnp.concatenate(
            [jnp.broadcast_to(x[c : c + 1], (DH, DH)).T for c in range(rows)], axis=0
        )

    inverse = upright(inverse_rows)
    pull = upright(pull_rows)
    for h in range(heads):
        cols = slice(h * DH, (h + 1) * DH)
        out = out_ref[:, cols]
        gain_h = gain[:, cols]
        normed = (gain_h * out * inverse).astype(BF16)
        normed_ref[:, cols] = normed
        weighted = gain_h * (normed.astype(F32) - t_ref[:, cols].astype(F32))
        grad = (weighted * inverse - out * pull).astype(BF16)
        go_ref[:, cols] = grad
        put_state(1, h, contract(keep(in_first, head(q_ref, h)).astype(BF16), grad, TN))
    gather_states(1)

    def mix(h):
        mixing = contract(head(go_ref, h), head(v_ref, h), NT)
        mix_ref[h] = jnp.where(same_doc, mixing, 0.0).astype(BF16)

    def query_grad(h):
        far_part = contract(head(go_ref, h), take_state(0, h), NT)
        near = contract(mix_ref[h], head(k_ref, h), NN)
        gq_ref[:, h * DH : (h + 1) * DH] = (near + keep(use_in, far_part)).astype(BF16)

    def near_grads(h):
        return (
            contract(mix_ref[h], head(q_ref, h), TN),
            contract(attn_ref[h], head(go_ref, h), TN),
        )

    for h in range(heads):
        mix(h)
        query_grad(h)
    fold_column(1)
    hand_out(1)
    near = [near_grads(h) for h in range(heads)]
    wait_slices(1, 1)
    for h in range(heads):
        suffix = take_state(1, h)
        cols = slice(h * DH, (h + 1) * DH)
        far_k = contract(head(v_ref, h), suffix, NT)
        far_v = contract(head(k_ref, h), suffix, NN)
        gk_ref[:, cols] = (near[h][0] + keep(use_out, far_k)).astype(BF16)
        gv_ref[:, cols] = (near[h][1] + keep(use_out, far_v)).astype(BF16)


def flush(*refs):
    *arrays, sem = refs
    n = len(arrays) // 2
    copies = [pltpu.make_async_copy(arrays[i], arrays[n + i], sem.at[i]) for i in range(n)]
    for copy in copies:
        copy.start()
    for copy in copies:
        copy.wait()


def solution(mesh):
    seqs, zs = mesh.shape["seq"], mesh.shape["head"]

    def per_device(queries, key_feats, value_feats, targets, norm_gain, doc_lengths):
        tok, width = queries.shape
        ring = MAXDOC // tok
        heads = width // DH
        slices = width // ring
        states = pltpu.VMEM((2, ring, slices, DH), F32)
        vmem = pl.BlockSpec(memory_space=pltpu.VMEM)
        hbm = pl.BlockSpec(memory_space=pltpu.HBM)
        block = pltpu.VMEM((tok, width), BF16)
        held = (
            pl.pallas_call(
                functools.partial(kernel, seqs, ring, zs),
                out_shape=[pltpu.VMEM((tok, width), BF16)] * 4,
                in_specs=[hbm] * 6,
                out_specs=[vmem] * 4,
                scratch_shapes=[
                    pltpu.SMEM(doc_lengths.shape, jnp.int32),
                    block,
                    block,
                    block,
                    block,
                    pltpu.VMEM((1, width), F32),
                    pltpu.VMEM((2, ring, DH), F32),
                    states,
                    states,
                    pltpu.VMEM((2, slices, DH), F32),
                    pltpu.VMEM((2, slices, DH), F32),
                    states,
                    states,
                    pltpu.VMEM((heads, tok, tok), BF16),
                    pltpu.VMEM((heads, tok, tok), BF16),
                    pltpu.VMEM((tok, width), F32),
                    pltpu.VMEM((tok, width), BF16),
                    pltpu.VMEM((3 * tok // DH, DH), F32),
                    pltpu.VMEM((zs, 3 * tok // DH, DH), F32),
                    pltpu.SemaphoreType.DMA((6,)),
                    pltpu.SemaphoreType.DMA((2, 2, ring)),
                    pltpu.SemaphoreType.DMA((2, 2, ring)),
                    pltpu.SemaphoreType.DMA((2, 2)),
                    pltpu.SemaphoreType.DMA((zs,)),
                    pltpu.SemaphoreType.DMA((zs,)),
                ],
                compiler_params=pltpu.CompilerParams(
                    collective_id=0, has_side_effects=True, vmem_limit_bytes=40 * 2**20
                ),
            )(
                *(
                    pltpu.with_memory_space_constraint(x, pltpu.HBM)
                    for x in (
                        doc_lengths,
                        queries,
                        key_feats,
                        value_feats,
                        targets,
                        norm_gain.reshape(1, width),
                    )
                )
            )
        )
        return tuple(
            pl.pallas_call(
                flush,
                out_shape=[jax.ShapeDtypeStruct((tok, width), BF16)] * 4,
                in_specs=[vmem] * 4,
                out_specs=[hbm] * 4,
                scratch_shapes=[pltpu.SemaphoreType.DMA((4,))],
                compiler_params=pltpu.CompilerParams(vmem_limit_bytes=8 * 2**20),
            )(*held)
        )

    spec = P("seq", "head")
    return jax.shard_map(
        per_device,
        mesh=mesh,
        in_specs=(spec, spec, spec, spec, P("head"), P()),
        out_specs=(spec, spec, spec, spec),
        check_vma=False,
    )
```

```python
import functools

import jax
import jax.numpy as jnp
from jax import lax
from jax.experimental import pallas as pl
from jax.experimental.pallas import tpu as pltpu
from jax.sharding import PartitionSpec as P

DH = 128
MAXDOC = 8192
MESH = pl.DeviceIdType.MESH
F32 = jnp.float32
BF16 = jnp.bfloat16


def contract(a, b, dims):
    return lax.dot_general(a, b, (dims, ((), ())), preferred_element_type=F32)


NN = ((1,), (0,))
NT = ((1,), (1,))
TN = ((0,), (0,))


def far_first(n):
    return sorted(range(1, n), key=lambda i: -min(i, n - i))


def kernel(
    seqs, ring, zs, len_in,
    q_in, k_in, v_in, t_in, g_in,
    normed_ref, gq_ref, gk_ref, gv_ref,
    len_ref, q_ref, k_ref, v_ref, t_ref, g_ref, flag_ref, through_ref, loc_ref, gat_ref, pre_ref, tot_ref, totin_ref, car_ref, carin_ref,
    attn_ref, mix_ref, out_ref, go_ref, sums_ref, sumsin_ref,
    load_sem, ssem, rsem, tsem, zsend, zrecv,
):
    tok, width = q_ref.shape
    heads = width // DH
    rows = tok // DH
    width_all = width * zs
    groups = seqs // ring
    docs = len_ref.shape[0]
    device = lax.axis_index("seq")
    z = lax.axis_index("head")
    place = lax.rem(device, ring)
    group = device // ring
    base = group * ring
    after = lax.rem(device + ring, seqs)
    before = lax.rem(device + seqs - ring, seqs)

    barrier = pltpu.get_barrier_semaphore()

    for i in far_first(zs):
        pl.semaphore_signal(
            barrier, inc=1, device_id=(device, lax.rem(z + i, zs)), device_id_type=MESH
        )
    for i in far_first(ring):
        pl.semaphore_signal(
            barrier, inc=1, device_id=(base + lax.rem(place + i, ring), z), device_id_type=MESH
        )
    pl.semaphore_signal(barrier, inc=1, device_id=(after, z), device_id_type=MESH)
    pl.semaphore_signal(barrier, inc=1, device_id=(before, z), device_id_type=MESH)

    loads = [
        pltpu.make_async_copy(src, dst, load_sem.at[i])
        for i, (src, dst) in enumerate(
            (
                (len_in, len_ref),
                (k_in, k_ref),
                (v_in, v_ref),
                (q_in, q_ref),
                (t_in, t_ref),
                (g_in, g_ref),
            )
        )
    ]
    for load in loads:
        load.start()
    loads[0].wait()

    ends = []
    total = jnp.int32(0)
    for d in range(docs):
        total = total + len_ref[d]
        ends.append(total)
    first = device * tok
    last = first + tok - 1
    far = jnp.int32(2**30)
    start_last = jnp.int32(0)
    start_next = jnp.int32(0)
    end_first = far
    end_prev = far
    for e in ends:
        start_last = jnp.where(e <= last, e, start_last)
        start_next = jnp.where(e <= last + 1, e, start_next)
    for e in reversed(ends):
        end_first = jnp.where(e > first, e, end_first)
        end_prev = jnp.where(e > first - 1, e, end_prev)

    def per_row(shape):
        return first + lax.broadcasted_iota(jnp.int32, shape, 0)

    row_pos = per_row((tok, DH))
    in_last = row_pos >= start_last
    in_first = row_pos < end_first
    use_in = row_pos < end_prev
    use_out = row_pos >= start_next

    def head(ref, h):
        return ref[:, h * DH : (h + 1) * DH]

    def keep(mask, x):
        return jnp.where(mask, x.astype(F32), 0.0)

    slices = heads * DH // ring

    def put_state(which, h, state):
        per_head = DH // slices
        loc_ref[which, h * per_head : (h + 1) * per_head] = state.reshape(per_head, slices, DH)

    loads[1].wait()
    loads[2].wait()
    for h in range(heads):
        put_state(0, h, contract(keep(in_last, head(k_ref, h)).astype(BF16), head(v_ref, h), TN))

    block_first = (base + lax.broadcasted_iota(jnp.int32, (ring, DH), 0)) * tok
    cut_f = jnp.zeros((ring, DH), jnp.int32)
    cut_r = jnp.zeros((ring, DH), jnp.int32)
    for e in ends:
        cut_f = cut_f | jnp.where((e >= block_first) & (e < block_first + tok), 1, 0)
        cut_r = cut_r | jnp.where((e > block_first) & (e <= block_first + tok), 1, 0)
    flag_ref[0] = 1.0 - cut_f.astype(F32)
    flag_ref[1] = 1.0 - cut_r.astype(F32)

    column_pos = first + lax.broadcasted_iota(jnp.int32, (1, tok), 1)
    end_of = jnp.full((1, tok), far, jnp.int32)
    for e in reversed(ends):
        end_of = jnp.where(e > column_pos, e, end_of)
    tall = per_row((tok, tok))
    wide = first + lax.broadcasted_iota(jnp.int32, (tok, tok), 1)
    same_doc = (tall >= wide) & (tall < end_of)

    def slice_copy(which, stage, i):
        src, dst = ((loc_ref, gat_ref), (car_ref, carin_ref))[stage]
        peer = lax.rem(place + i, ring)
        return pltpu.make_async_remote_copy(
            src_ref=src.at[which, peer],
            dst_ref=dst.at[which, place],
            send_sem=ssem.at[which, stage, i],
            recv_sem=rsem.at[which, stage, i],
            device_id=(base + peer, z),
            device_id_type=MESH,
        )

    def start_slices(which, stage):
        for i in far_first(ring):
            slice_copy(which, stage, i).start()

    def wait_slices(which, stage):
        for i in reversed(far_first(ring)):
            slice_copy(which, stage, i).wait_recv()

    def wait_sent(which, stage):
        def one(i, carry):
            slice_copy(which, stage, i).wait_send()
            return carry

        lax.fori_loop(1, ring, one, 0)

    def total_copy(which):
        return pltpu.make_async_remote_copy(
            src_ref=tot_ref.at[which],
            dst_ref=totin_ref.at[which],
            send_sem=tsem.at[which, 0],
            recv_sem=tsem.at[which, 1],
            device_id=(before if which else after, z),
            device_id_type=MESH,
        )

    def order(which):
        return reversed(range(ring)) if which else range(ring)

    def gather_states(which):
        start_slices(which, 0)
        gat_ref[which, place] = loc_ref[which, place]

    def fold_column(which):
        wait_slices(which, 0)
        run = jnp.zeros((slices, DH), F32)
        for j in order(which):
            pre_ref[which, j] = run
            run = gat_ref[which, j] + flag_ref[which, j : j + 1] * run
        tot_ref[which] = run
        total_copy(which).start()
        through = jnp.ones((1, DH), F32)
        for j in order(which):
            through_ref[which, j : j + 1] = through
            through = through * flag_ref[which, j : j + 1]

    def hand_out(which):
        total_copy(which).wait_recv()
        inside = group < groups - 1 if which else group > 0
        run = jnp.where(inside, totin_ref[which], 0.0)
        for j in range(ring):
            car_ref[which, j] = pre_ref[which, j] + through_ref[which, j : j + 1] * run
        start_slices(which, 1)
        carin_ref[which, place] = car_ref[which, place]
        total_copy(which).wait_send()
        wait_sent(which, 0)

    def take_state(which, h):
        per_head = DH // slices
        part = carin_ref[which, h * per_head : (h + 1) * per_head]
        return part.reshape(DH, DH).astype(BF16)

    def attend(h):
        scores = contract(head(q_ref, h), head(k_ref, h), NT)
        attn_ref[h] = jnp.where(same_doc, scores, 0.0).astype(BF16)

    def local_output(h):
        out_ref[:, h * DH : (h + 1) * DH] = contract(attn_ref[h], head(v_ref, h), NN)

    pl.semaphore_wait(barrier, ring + zs)
    gather_states(0)
    loads[3].wait()
    loads[4].wait()
    loads[5].wait()
    for h in range(heads):
        attend(h)
    for h in range(heads):
        local_output(h)
    fold_column(0)
    hand_out(0)
    wait_slices(0, 1)

    gain = g_ref[...]
    squares = jnp.zeros((tok, DH), F32)
    gained = jnp.zeros((tok, DH), F32)
    crossed = jnp.zeros((tok, DH), F32)
    for h in range(heads):
        out = head(out_ref, h) + keep(use_in, contract(head(q_ref, h), take_state(0, h), NN))
        out_ref[:, h * DH : (h + 1) * DH] = out
        scaled = gain[:, h * DH : (h + 1) * DH] * out
        squares = squares + out * out
        gained = gained + scaled * scaled
        crossed = crossed + scaled * head(t_ref, h).astype(F32)
    lane = lax.broadcasted_iota(jnp.int32, (tok, DH), 1)
    packed = jnp.where(
        lane == 0,
        jnp.sum(squares, axis=1, keepdims=True),
        jnp.where(
            lane == 1,
            jnp.sum(gained, axis=1, keepdims=True),
            jnp.sum(crossed, axis=1, keepdims=True),
        ),
    )
    for c in range(rows):
        turned = packed[c * DH : (c + 1) * DH].T
        for r in range(3):
            sums_ref[r * rows + c : r * rows + c + 1] = turned[r : r + 1]
    sumsin_ref[z] = sums_ref[...]

    def sum_copy(i):
        return pltpu.make_async_remote_copy(
            src_ref=sums_ref,
            dst_ref=sumsin_ref.at[z],
            send_sem=zsend.at[i],
            recv_sem=zrecv.at[i],
            device_id=(device, lax.rem(z + i, zs)),
            device_id_type=MESH,
        )

    for i in far_first(zs):
        sum_copy(i).start()
    wait_sent(0, 1)
    for i in reversed(far_first(zs)):
        sum_copy(i).wait_recv()
    summed = sumsin_ref[0]
    for i in range(1, zs):
        summed = summed + sumsin_ref[i]
    inverse_rows = lax.rsqrt(summed[0:rows] / width_all + 1e-06)
    slope_rows = inverse_rows * summed[rows : 2 * rows] - summed[2 * rows : 3 * rows]
    pull_rows = slope_rows * (inverse_rows * inverse_rows * inverse_rows) / width_all

    def upright(x):
        return jnp.concatenate(
            [jnp.broadcast_to(x[c : c + 1], (DH, DH)).T for c in range(rows)], axis=0
        )

    inverse = upright(inverse_rows)
    pull = upright(pull_rows)
    for h in range(heads):
        cols = slice(h * DH, (h + 1) * DH)
        out = out_ref[:, cols]
        gain_h = gain[:, cols]
        normed = (gain_h * out * inverse).astype(BF16)
        normed_ref[:, cols] = normed
        weighted = gain_h * (normed.astype(F32) - t_ref[:, cols].astype(F32))
        grad = (weighted * inverse - out * pull).astype(BF16)
        go_ref[:, cols] = grad
        put_state(1, h, contract(keep(in_first, head(q_ref, h)).astype(BF16), grad, TN))
    gather_states(1)

    def mix(h):
        mixing = contract(head(go_ref, h), head(v_ref, h), NT)
        mix_ref[h] = jnp.where(same_doc, mixing, 0.0).astype(BF16)

    def query_grad(h):
        far_part = contract(head(go_ref, h), take_state(0, h), NT)
        near = contract(mix_ref[h], head(k_ref, h), NN)
        gq_ref[:, h * DH : (h + 1) * DH] = (near + keep(use_in, far_part)).astype(BF16)

    def near_grads(h):
        return (
            contract(mix_ref[h], head(q_ref, h), TN),
            contract(attn_ref[h], head(go_ref, h), TN),
        )

    for h in range(heads):
        mix(h)
        query_grad(h)
    fold_column(1)
    hand_out(1)
    near = [near_grads(h) for h in range(heads)]
    for i in range(1, zs):
        sum_copy(i).wait_send()
    wait_slices(1, 1)
    for h in range(heads):
        suffix = take_state(1, h)
        cols = slice(h * DH, (h + 1) * DH)
        far_k = contract(head(v_ref, h), suffix, NT)
        far_v = contract(head(k_ref, h), suffix, NN)
        gk_ref[:, cols] = (near[h][0] + keep(use_out, far_k)).astype(BF16)
        gv_ref[:, cols] = (near[h][1] + keep(use_out, far_v)).astype(BF16)
    wait_sent(1, 1)


def flush(*refs):
    *arrays, sem = refs
    n = len(arrays) // 2
    copies = [pltpu.make_async_copy(arrays[i], arrays[n + i], sem.at[i]) for i in range(n)]
    for copy in copies:
        copy.start()
    for copy in copies:
        copy.wait()


def solution(mesh):
    seqs, zs = mesh.shape["seq"], mesh.shape["head"]

    def per_device(queries, key_feats, value_feats, targets, norm_gain, doc_lengths):
        tok, width = queries.shape
        ring = MAXDOC // tok
        heads = width // DH
        slices = width // ring
        states = pltpu.VMEM((2, ring, slices, DH), F32)
        vmem = pl.BlockSpec(memory_space=pltpu.VMEM)
        hbm = pl.BlockSpec(memory_space=pltpu.HBM)
        block = pltpu.VMEM((tok, width), BF16)
        held = (
            pl.pallas_call(
                functools.partial(kernel, seqs, ring, zs),
                out_shape=[pltpu.VMEM((tok, width), BF16)] * 4,
                in_specs=[hbm] * 6,
                out_specs=[vmem] * 4,
                scratch_shapes=[
                    pltpu.SMEM(doc_lengths.shape, jnp.int32),
                    block,
                    block,
                    block,
                    block,
                    pltpu.VMEM((1, width), F32),
                    pltpu.VMEM((2, ring, DH), F32),
                    pltpu.VMEM((2, ring, DH), F32),
                    states,
                    states,
                    states,
                    pltpu.VMEM((2, slices, DH), F32),
                    pltpu.VMEM((2, slices, DH), F32),
                    states,
                    states,
                    pltpu.VMEM((heads, tok, tok), BF16),
                    pltpu.VMEM((heads, tok, tok), BF16),
                    pltpu.VMEM((tok, width), F32),
                    pltpu.VMEM((tok, width), BF16),
                    pltpu.VMEM((3 * tok // DH, DH), F32),
                    pltpu.VMEM((zs, 3 * tok // DH, DH), F32),
                    pltpu.SemaphoreType.DMA((6,)),
                    pltpu.SemaphoreType.DMA((2, 2, ring)),
                    pltpu.SemaphoreType.DMA((2, 2, ring)),
                    pltpu.SemaphoreType.DMA((2, 2)),
                    pltpu.SemaphoreType.DMA((zs,)),
                    pltpu.SemaphoreType.DMA((zs,)),
                ],
                compiler_params=pltpu.CompilerParams(
                    collective_id=0, has_side_effects=True, vmem_limit_bytes=40 * 2**20
                ),
            )(
                *(
                    pltpu.with_memory_space_constraint(x, pltpu.HBM)
                    for x in (
                        doc_lengths,
                        queries,
                        key_feats,
                        value_feats,
                        targets,
                        norm_gain.reshape(1, width),
                    )
                )
            )
        )
        return tuple(
            pl.pallas_call(
                flush,
                out_shape=[jax.ShapeDtypeStruct((tok, width), BF16)] * 4,
                in_specs=[vmem] * 4,
                out_specs=[hbm] * 4,
                scratch_shapes=[pltpu.SemaphoreType.DMA((4,))],
                compiler_params=pltpu.CompilerParams(vmem_limit_bytes=8 * 2**20),
            )(*held)
        )

    spec = P("seq", "head")
    return jax.shard_map(
        per_device,
        mesh=mesh,
        in_specs=(spec, spec, spec, spec, P("head"), P()),
        out_specs=(spec, spec, spec, spec),
        check_vma=False,
    )
```

```python
import functools

import jax
import jax.numpy as jnp
from jax import lax
from jax.experimental import pallas as pl
from jax.experimental.pallas import tpu as pltpu
from jax.sharding import PartitionSpec as P

DH = 128
MAXDOC = 8192
MESH = pl.DeviceIdType.MESH
F32 = jnp.float32
BF16 = jnp.bfloat16


def contract(a, b, dims):
    return lax.dot_general(a, b, (dims, ((), ())), preferred_element_type=F32)


NN = ((1,), (0,))
NT = ((1,), (1,))
TN = ((0,), (0,))


def far_first(n):
    return sorted(range(1, n), key=lambda i: -min(i, n - i))


def kernel(
    seqs, ring, zs, len_in,
    q_in, k_in, v_in, t_in, g_in,
    normed_ref, gq_ref, gk_ref, gv_ref,
    len_ref, q_ref, k_ref, v_ref, t_ref, g_ref, flag_ref, through_ref, loc_ref, gat_ref, pre_ref, tot_ref, totin_ref, car_ref, carin_ref,
    turned_ref, attn_ref, mix_ref, out_ref, go_ref, sums_ref, sumsin_ref,
    load_sem, ssem, rsem, tsem, zsend, zrecv,
):
    tok, width = q_ref.shape
    heads = width // DH
    rows = tok // DH
    width_all = width * zs
    groups = seqs // ring
    docs = len_ref.shape[0]
    device = lax.axis_index("seq")
    z = lax.axis_index("head")
    place = lax.rem(device, ring)
    group = device // ring
    base = group * ring
    after = lax.rem(device + ring, seqs)
    before = lax.rem(device + seqs - ring, seqs)

    loads = [
        pltpu.make_async_copy(src, dst, load_sem.at[i])
        for i, (src, dst) in enumerate(
            (
                (len_in, len_ref),
                (k_in, k_ref),
                (v_in, v_ref),
                (q_in, q_ref),
                (t_in, t_ref),
                (g_in, g_ref),
            )
        )
    ]
    for load in loads:
        load.start()

    barrier = pltpu.get_barrier_semaphore()

    for i in far_first(zs):
        pl.semaphore_signal(
            barrier, inc=1, device_id=(device, lax.rem(z + i, zs)), device_id_type=MESH
        )
    for i in far_first(ring):
        pl.semaphore_signal(
            barrier, inc=1, device_id=(base + lax.rem(place + i, ring), z), device_id_type=MESH
        )
    pl.semaphore_signal(barrier, inc=1, device_id=(after, z), device_id_type=MESH)
    pl.semaphore_signal(barrier, inc=1, device_id=(before, z), device_id_type=MESH)

    loads[0].wait()

    ends = []
    total = jnp.int32(0)
    for d in range(docs):
        total = total + len_ref[d]
        ends.append(total)
    first = device * tok
    last = first + tok - 1
    far = jnp.int32(2**30)
    start_last = jnp.int32(0)
    start_next = jnp.int32(0)
    end_first = far
    end_prev = far
    for e in ends:
        start_last = jnp.where(e <= last, e, start_last)
        start_next = jnp.where(e <= last + 1, e, start_next)
    for e in reversed(ends):
        end_first = jnp.where(e > first, e, end_first)
        end_prev = jnp.where(e > first - 1, e, end_prev)

    def per_row(shape):
        return first + lax.broadcasted_iota(jnp.int32, shape, 0)

    row_pos = per_row((tok, DH))
    in_last = row_pos >= start_last
    in_first = row_pos < end_first
    use_in = row_pos < end_prev
    use_out = row_pos >= start_next

    def head(ref, h):
        return ref[:, h * DH : (h + 1) * DH]

    def keep(mask, x):
        return jnp.where(mask, x.astype(F32), 0.0)

    slices = heads * DH // ring

    def put_state(which, h, state):
        per_head = DH // slices
        loc_ref[which, h * per_head : (h + 1) * per_head] = state.reshape(per_head, slices, DH)

    loads[1].wait()
    loads[2].wait()
    for h in range(heads):
        put_state(0, h, contract(keep(in_last, head(k_ref, h)).astype(BF16), head(v_ref, h), TN))

    block_first = (base + lax.broadcasted_iota(jnp.int32, (ring, DH), 0)) * tok
    cut_f = jnp.zeros((ring, DH), jnp.int32)
    cut_r = jnp.zeros((ring, DH), jnp.int32)
    for e in ends:
        cut_f = cut_f | jnp.where((e >= block_first) & (e < block_first + tok), 1, 0)
        cut_r = cut_r | jnp.where((e > block_first) & (e <= block_first + tok), 1, 0)
    flag_ref[0] = 1.0 - cut_f.astype(F32)
    flag_ref[1] = 1.0 - cut_r.astype(F32)

    column_pos = first + lax.broadcasted_iota(jnp.int32, (1, tok), 1)
    end_of = jnp.full((1, tok), far, jnp.int32)
    for e in reversed(ends):
        end_of = jnp.where(e > column_pos, e, end_of)
    tall = per_row((tok, tok))
    wide = first + lax.broadcasted_iota(jnp.int32, (tok, tok), 1)
    same_doc = (tall >= wide) & (tall < end_of)

    def slice_copy(which, stage, i):
        src, dst = ((loc_ref, gat_ref), (car_ref, carin_ref))[stage]
        peer = lax.rem(place + i, ring)
        return pltpu.make_async_remote_copy(
            src_ref=src.at[which, peer],
            dst_ref=dst.at[which, place],
            send_sem=ssem.at[which, stage, i],
            recv_sem=rsem.at[which, stage, i],
            device_id=(base + peer, z),
            device_id_type=MESH,
        )

    def start_slices(which, stage):
        for i in far_first(ring):
            slice_copy(which, stage, i).start()

    def wait_slices(which, stage):
        for i in reversed(far_first(ring)):
            slice_copy(which, stage, i).wait_recv()

    def wait_sent(which, stage):
        def one(i, carry):
            slice_copy(which, stage, i).wait_send()
            return carry

        lax.fori_loop(1, ring, one, 0)

    def total_copy(which):
        return pltpu.make_async_remote_copy(
            src_ref=tot_ref.at[which],
            dst_ref=totin_ref.at[which],
            send_sem=tsem.at[which, 0],
            recv_sem=tsem.at[which, 1],
            device_id=(before if which else after, z),
            device_id_type=MESH,
        )

    def gives(which):
        return group > 0 if which else group < groups - 1

    def order(which):
        return reversed(range(ring)) if which else range(ring)

    def gather_states(which):
        start_slices(which, 0)
        gat_ref[which, place] = loc_ref[which, place]

    def fold_column(which):
        wait_slices(which, 0)
        run = jnp.zeros((slices, DH), F32)
        for j in order(which):
            pre_ref[which, j] = run
            run = gat_ref[which, j] + flag_ref[which, j : j + 1] * run
        tot_ref[which] = run

        @pl.when(gives(which))
        def _():
            total_copy(which).start()

        through = jnp.ones((1, DH), F32)
        for j in order(which):
            through_ref[which, j : j + 1] = through
            through = through * flag_ref[which, j : j + 1]

    def hand_out(which):
        @pl.when(gives(1 - which))
        def _():
            total_copy(which).wait_recv()

        @pl.when(jnp.logical_not(gives(1 - which)))
        def _():
            totin_ref[which] = jnp.zeros((slices, DH), F32)

        run = totin_ref[which]
        for j in range(ring):
            car_ref[which, j] = pre_ref[which, j] + through_ref[which, j : j + 1] * run
        start_slices(which, 1)
        carin_ref[which, place] = car_ref[which, place]

        @pl.when(gives(which))
        def _():
            total_copy(which).wait_send()

        wait_sent(which, 0)

    def take_state(which, h):
        per_head = DH // slices
        part = carin_ref[which, h * per_head : (h + 1) * per_head]
        return part.reshape(DH, DH).astype(BF16)

    def attend(h):
        scores = contract(head(q_ref, h), head(k_ref, h), NT)
        attn_ref[h] = jnp.where(same_doc, scores, 0.0).astype(BF16)

    def local_output(h):
        out_ref[:, h * DH : (h + 1) * DH] = contract(attn_ref[h], head(v_ref, h), NN)

    pl.semaphore_wait(barrier, ring + zs)
    gather_states(0)
    loads[3].wait()
    loads[4].wait()
    loads[5].wait()
    for h in range(heads):
        attend(h)
    for h in range(heads):
        local_output(h)
    fold_column(0)
    hand_out(0)
    wait_slices(0, 1)

    gain = g_ref[...]
    squares = jnp.zeros((tok, DH), F32)
    gained = jnp.zeros((tok, DH), F32)
    crossed = jnp.zeros((tok, DH), F32)
    for h in range(heads):
        out = head(out_ref, h) + keep(use_in, contract(head(q_ref, h), take_state(0, h), NN))
        out_ref[:, h * DH : (h + 1) * DH] = out
        scaled = gain[:, h * DH : (h + 1) * DH] * out
        squares = squares + out * out
        gained = gained + scaled * scaled
        crossed = crossed + scaled * head(t_ref, h).astype(F32)
    lane = lax.broadcasted_iota(jnp.int32, (tok, DH), 1)
    packed = jnp.where(
        lane == 0,
        jnp.sum(squares, axis=1, keepdims=True),
        jnp.where(
            lane == 1,
            jnp.sum(gained, axis=1, keepdims=True),
            jnp.sum(crossed, axis=1, keepdims=True),
        ),
    )
    for c in range(rows):
        turned = packed[c * DH : (c + 1) * DH].T
        for r in range(3):
            sums_ref[r * rows + c : r * rows + c + 1] = turned[r : r + 1]
    sumsin_ref[z] = sums_ref[...]

    def sum_copy(i):
        return pltpu.make_async_remote_copy(
            src_ref=sums_ref,
            dst_ref=sumsin_ref.at[z],
            send_sem=zsend.at[i],
            recv_sem=zrecv.at[i],
            device_id=(device, lax.rem(z + i, zs)),
            device_id_type=MESH,
        )

    for i in far_first(zs):
        sum_copy(i).start()
    wait_sent(0, 1)
    for h in range(heads):
        turned_ref[h] = keep(in_first, head(q_ref, h)).T.astype(BF16)
    for i in reversed(far_first(zs)):
        sum_copy(i).wait_recv()
    summed = sumsin_ref[0]
    for i in range(1, zs):
        summed = summed + sumsin_ref[i]
    inverse_rows = lax.rsqrt(summed[0:rows] / width_all + 1e-06)
    slope_rows = inverse_rows * summed[rows : 2 * rows] - summed[2 * rows : 3 * rows]
    pull_rows = slope_rows * (inverse_rows * inverse_rows * inverse_rows) / width_all

    def upright(x):
        return jnp.concatenate(
            [jnp.broadcast_to(x[c : c + 1], (DH, DH)).T for c in range(rows)], axis=0
        )

    inverse = upright(inverse_rows)
    pull = upright(pull_rows)
    for h in range(heads):
        cols = slice(h * DH, (h + 1) * DH)
        out = out_ref[:, cols]
        gain_h = gain[:, cols]
        normed = (gain_h * out * inverse).astype(BF16)
        normed_ref[:, cols] = normed
        weighted = gain_h * (normed.astype(F32) - t_ref[:, cols].astype(F32))
        grad = (weighted * inverse - out * pull).astype(BF16)
        go_ref[:, cols] = grad
        put_state(1, h, contract(turned_ref[h], grad, NN))
    gather_states(1)

    def mix(h):
        mixing = contract(head(go_ref, h), head(v_ref, h), NT)
        mix_ref[h] = jnp.where(same_doc, mixing, 0.0).astype(BF16)

    def query_grad(h):
        far_part = contract(head(go_ref, h), take_state(0, h), NT)
        near = contract(mix_ref[h], head(k_ref, h), NN)
        gq_ref[:, h * DH : (h + 1) * DH] = (near + keep(use_in, far_part)).astype(BF16)

    def near_grads(h):
        return (
            contract(mix_ref[h], head(q_ref, h), TN),
            contract(attn_ref[h], head(go_ref, h), TN),
        )

    for h in range(heads):
        mix(h)
        query_grad(h)
    fold_column(1)
    hand_out(1)
    near = [near_grads(h) for h in range(heads)]
    for i in range(1, zs):
        sum_copy(i).wait_send()
    wait_slices(1, 1)
    for h in range(heads):
        suffix = take_state(1, h)
        cols = slice(h * DH, (h + 1) * DH)
        far_k = contract(head(v_ref, h), suffix, NT)
        far_v = contract(head(k_ref, h), suffix, NN)
        gk_ref[:, cols] = (near[h][0] + keep(use_out, far_k)).astype(BF16)
        gv_ref[:, cols] = (near[h][1] + keep(use_out, far_v)).astype(BF16)
    wait_sent(1, 1)


def flush(*refs):
    *arrays, sem = refs
    n = len(arrays) // 2
    copies = [pltpu.make_async_copy(arrays[i], arrays[n + i], sem.at[i]) for i in range(n)]
    for copy in copies:
        copy.start()
    for copy in copies:
        copy.wait()


def solution(mesh):
    seqs, zs = mesh.shape["seq"], mesh.shape["head"]

    def per_device(queries, key_feats, value_feats, targets, norm_gain, doc_lengths):
        tok, width = queries.shape
        ring = MAXDOC // tok
        heads = width // DH
        slices = width // ring
        states = pltpu.VMEM((2, ring, slices, DH), F32)
        vmem = pl.BlockSpec(memory_space=pltpu.VMEM)
        hbm = pl.BlockSpec(memory_space=pltpu.HBM)
        block = pltpu.VMEM((tok, width), BF16)
        held = (
            pl.pallas_call(
                functools.partial(kernel, seqs, ring, zs),
                out_shape=[pltpu.VMEM((tok, width), BF16)] * 4,
                in_specs=[hbm] * 6,
                out_specs=[vmem] * 4,
                scratch_shapes=[
                    pltpu.SMEM(doc_lengths.shape, jnp.int32),
                    block,
                    block,
                    block,
                    block,
                    pltpu.VMEM((1, width), F32),
                    pltpu.VMEM((2, ring, DH), F32),
                    pltpu.VMEM((2, ring, DH), F32),
                    states,
                    states,
                    states,
                    pltpu.VMEM((2, slices, DH), F32),
                    pltpu.VMEM((2, slices, DH), F32),
                    states,
                    states,
                    pltpu.VMEM((heads, DH, tok), BF16),
                    pltpu.VMEM((heads, tok, tok), BF16),
                    pltpu.VMEM((heads, tok, tok), BF16),
                    pltpu.VMEM((tok, width), F32),
                    pltpu.VMEM((tok, width), BF16),
                    pltpu.VMEM((3 * tok // DH, DH), F32),
                    pltpu.VMEM((zs, 3 * tok // DH, DH), F32),
                    pltpu.SemaphoreType.DMA((6,)),
                    pltpu.SemaphoreType.DMA((2, 2, ring)),
                    pltpu.SemaphoreType.DMA((2, 2, ring)),
                    pltpu.SemaphoreType.DMA((2, 2)),
                    pltpu.SemaphoreType.DMA((zs,)),
                    pltpu.SemaphoreType.DMA((zs,)),
                ],
                compiler_params=pltpu.CompilerParams(
                    collective_id=0, has_side_effects=True, vmem_limit_bytes=40 * 2**20
                ),
            )(
                *(
                    pltpu.with_memory_space_constraint(x, pltpu.HBM)
                    for x in (
                        doc_lengths,
                        queries,
                        key_feats,
                        value_feats,
                        targets,
                        norm_gain.reshape(1, width),
                    )
                )
            )
        )
        return tuple(
            pl.pallas_call(
                flush,
                out_shape=[jax.ShapeDtypeStruct((tok, width), BF16)] * 4,
                in_specs=[vmem] * 4,
                out_specs=[hbm] * 4,
                scratch_shapes=[pltpu.SemaphoreType.DMA((4,))],
                compiler_params=pltpu.CompilerParams(vmem_limit_bytes=8 * 2**20),
            )(*held)
        )

    spec = P("seq", "head")
    return jax.shard_map(
        per_device,
        mesh=mesh,
        in_specs=(spec, spec, spec, spec, P("head"), P()),
        out_specs=(spec, spec, spec, spec),
        check_vma=False,
    )
```

```python
import functools

import jax
import jax.numpy as jnp
from jax import lax
from jax.experimental import pallas as pl
from jax.experimental.pallas import tpu as pltpu
from jax.sharding import PartitionSpec as P

DH = 128
MAXDOC = 8192
MESH = pl.DeviceIdType.MESH
F32 = jnp.float32
BF16 = jnp.bfloat16


def contract(a, b, dims):
    return lax.dot_general(a, b, (dims, ((), ())), preferred_element_type=F32)


NN = ((1,), (0,))
NT = ((1,), (1,))
TN = ((0,), (0,))


def far_first(n):
    return sorted(range(1, n), key=lambda i: -min(i, n - i))


def kernel(
    seqs, ring, zs, len_in,
    q_in, k_in, v_in, t_in, g_in,
    normed_ref, gq_ref, gk_ref, gv_ref,
    len_ref, q_ref, k_ref, v_ref, t_ref, g_ref, flag_ref, through_ref, loc_ref, gat_ref, pre_ref, tot_ref, totin_ref, car_ref, carin_ref,
    turned_ref, attn_ref, mix_ref, out_ref, go_ref, sums_ref, sumsin_ref,
    load_sem, ssem, rsem, tsem, zsend, zrecv,
):
    tok, width = q_ref.shape
    heads = width // DH
    rows = tok // DH
    width_all = width * zs
    groups = seqs // ring
    docs = len_ref.shape[0]
    device = lax.axis_index("seq")
    z = lax.axis_index("head")
    place = lax.rem(device, ring)
    group = device // ring
    base = group * ring
    after = lax.rem(device + ring, seqs)
    before = lax.rem(device + seqs - ring, seqs)

    loads = [
        pltpu.make_async_copy(src, dst, load_sem.at[i])
        for i, (src, dst) in enumerate(
            (
                (len_in, len_ref),
                (k_in, k_ref),
                (v_in, v_ref),
                (q_in, q_ref),
                (t_in, t_ref),
                (g_in, g_ref),
            )
        )
    ]
    for load in loads:
        load.start()

    barrier = pltpu.get_barrier_semaphore()

    for i in far_first(zs):
        pl.semaphore_signal(
            barrier, inc=1, device_id=(device, lax.rem(z + i, zs)), device_id_type=MESH
        )
    for i in far_first(ring):
        pl.semaphore_signal(
            barrier, inc=1, device_id=(base + lax.rem(place + i, ring), z), device_id_type=MESH
        )
    pl.semaphore_signal(barrier, inc=1, device_id=(after, z), device_id_type=MESH)
    pl.semaphore_signal(barrier, inc=1, device_id=(before, z), device_id_type=MESH)

    loads[0].wait()

    ends = []
    total = jnp.int32(0)
    for d in range(docs):
        total = total + len_ref[d]
        ends.append(total)
    first = device * tok
    last = first + tok - 1
    far = jnp.int32(2**30)
    start_last = jnp.int32(0)
    start_next = jnp.int32(0)
    end_first = far
    end_prev = far
    for e in ends:
        start_last = jnp.where(e <= last, e, start_last)
        start_next = jnp.where(e <= last + 1, e, start_next)
    for e in reversed(ends):
        end_first = jnp.where(e > first, e, end_first)
        end_prev = jnp.where(e > first - 1, e, end_prev)

    def per_row(shape):
        return first + lax.broadcasted_iota(jnp.int32, shape, 0)

    row_pos = per_row((tok, DH))
    in_last = row_pos >= start_last
    in_first = row_pos < end_first
    use_in = row_pos < end_prev
    use_out = row_pos >= start_next

    def head(ref, h):
        return ref[:, h * DH : (h + 1) * DH]

    def keep(mask, x):
        return jnp.where(mask, x.astype(F32), 0.0)

    slices = heads * DH // ring

    def put_state(which, h, state):
        per_head = DH // slices
        loc_ref[which, h * per_head : (h + 1) * per_head] = state.reshape(per_head, slices, DH)

    loads[1].wait()
    loads[2].wait()
    for h in range(heads):
        put_state(0, h, contract(keep(in_last, head(k_ref, h)).astype(BF16), head(v_ref, h), TN))

    block_first = (base + lax.broadcasted_iota(jnp.int32, (ring, DH), 0)) * tok
    cut_f = jnp.zeros((ring, DH), jnp.int32)
    cut_r = jnp.zeros((ring, DH), jnp.int32)
    for e in ends:
        cut_f = cut_f | jnp.where((e >= block_first) & (e < block_first + tok), 1, 0)
        cut_r = cut_r | jnp.where((e > block_first) & (e <= block_first + tok), 1, 0)
    flag_ref[0] = 1.0 - cut_f.astype(F32)
    flag_ref[1] = 1.0 - cut_r.astype(F32)

    column_pos = first + lax.broadcasted_iota(jnp.int32, (1, tok), 1)
    end_of = jnp.full((1, tok), far, jnp.int32)
    for e in reversed(ends):
        end_of = jnp.where(e > column_pos, e, end_of)
    tall = per_row((tok, tok))
    wide = first + lax.broadcasted_iota(jnp.int32, (tok, tok), 1)
    same_doc = (tall >= wide) & (tall < end_of)

    def slice_copy(which, stage, i):
        src, dst = ((loc_ref, gat_ref), (car_ref, carin_ref))[stage]
        peer = lax.rem(place + i, ring)
        return pltpu.make_async_remote_copy(
            src_ref=src.at[which, peer],
            dst_ref=dst.at[which, place],
            send_sem=ssem.at[which, stage, i],
            recv_sem=rsem.at[which, stage, i],
            device_id=(base + peer, z),
            device_id_type=MESH,
        )

    def start_slices(which, stage):
        for i in far_first(ring):
            slice_copy(which, stage, i).start()

    def wait_slices(which, stage):
        for i in reversed(far_first(ring)):
            slice_copy(which, stage, i).wait_recv()

    def wait_sent(which, stage):
        def one(i, carry):
            slice_copy(which, stage, i).wait_send()
            return carry

        lax.fori_loop(1, ring, one, 0)

    def total_copy(which):
        return pltpu.make_async_remote_copy(
            src_ref=tot_ref.at[which],
            dst_ref=totin_ref.at[which],
            send_sem=tsem.at[which, 0],
            recv_sem=tsem.at[which, 1],
            device_id=(before if which else after, z),
            device_id_type=MESH,
        )

    def gives(which):
        return group > 0 if which else group < groups - 1

    def order(which):
        return reversed(range(ring)) if which else range(ring)

    def gather_states(which):
        start_slices(which, 0)
        gat_ref[which, place] = loc_ref[which, place]

    def fold_column(which):
        wait_slices(which, 0)
        run = jnp.zeros((slices, DH), F32)
        for j in order(which):
            pre_ref[which, j] = run
            run = gat_ref[which, j] + flag_ref[which, j : j + 1] * run
        tot_ref[which] = run

        @pl.when(gives(which))
        def _():
            total_copy(which).start()

        through = jnp.ones((1, DH), F32)
        for j in order(which):
            through_ref[which, j : j + 1] = through
            through = through * flag_ref[which, j : j + 1]

    def hand_out(which):
        @pl.when(gives(1 - which))
        def _():
            total_copy(which).wait_recv()

        @pl.when(jnp.logical_not(gives(1 - which)))
        def _():
            totin_ref[which] = jnp.zeros((slices, DH), F32)

        run = totin_ref[which]
        for j in range(ring):
            car_ref[which, j] = pre_ref[which, j] + through_ref[which, j : j + 1] * run
        start_slices(which, 1)
        carin_ref[which, place] = car_ref[which, place]

        @pl.when(gives(which))
        def _():
            total_copy(which).wait_send()

        wait_sent(which, 0)

    def take_state(which, h):
        per_head = DH // slices
        part = carin_ref[which, h * per_head : (h + 1) * per_head]
        return part.reshape(DH, DH).astype(BF16)

    def attend(h):
        scores = contract(head(q_ref, h), head(k_ref, h), NT)
        attn_ref[h] = jnp.where(same_doc, scores, 0.0).astype(BF16)

    def local_output(h):
        out_ref[:, h * DH : (h + 1) * DH] = contract(attn_ref[h], head(v_ref, h), NN)

    pl.semaphore_wait(barrier, ring + zs)
    gather_states(0)
    loads[3].wait()
    loads[4].wait()
    loads[5].wait()
    for h in range(heads):
        attend(h)
    for h in range(heads):
        local_output(h)
    fold_column(0)
    hand_out(0)
    wait_slices(0, 1)

    gain = g_ref[...]
    squares = jnp.zeros((tok, DH), F32)
    gained = jnp.zeros((tok, DH), F32)
    crossed = jnp.zeros((tok, DH), F32)
    for h in range(heads):
        out = head(out_ref, h) + keep(use_in, contract(head(q_ref, h), take_state(0, h), NN))
        out_ref[:, h * DH : (h + 1) * DH] = out
        scaled = gain[:, h * DH : (h + 1) * DH] * out
        squares = squares + out * out
        gained = gained + scaled * scaled
        crossed = crossed + scaled * head(t_ref, h).astype(F32)
    for r, terms in enumerate((squares, gained, crossed)):
        for c in range(rows):
            turned = terms[c * DH : (c + 1) * DH].T
            sums_ref[r * rows + c : r * rows + c + 1] = jnp.sum(turned, axis=0, keepdims=True)
    sumsin_ref[z] = sums_ref[...]

    def sum_copy(i):
        return pltpu.make_async_remote_copy(
            src_ref=sums_ref,
            dst_ref=sumsin_ref.at[z],
            send_sem=zsend.at[i],
            recv_sem=zrecv.at[i],
            device_id=(device, lax.rem(z + i, zs)),
            device_id_type=MESH,
        )

    for i in far_first(zs):
        sum_copy(i).start()
    wait_sent(0, 1)
    for h in range(heads):
        turned_ref[h] = keep(in_first, head(q_ref, h)).T.astype(BF16)
    for i in reversed(far_first(zs)):
        sum_copy(i).wait_recv()
    summed = sumsin_ref[0]
    for i in range(1, zs):
        summed = summed + sumsin_ref[i]
    inverse_rows = lax.rsqrt(summed[0:rows] / width_all + 1e-06)
    slope_rows = inverse_rows * summed[rows : 2 * rows] - summed[2 * rows : 3 * rows]
    pull_rows = slope_rows * (inverse_rows * inverse_rows * inverse_rows) / width_all

    def upright(x):
        return jnp.concatenate(
            [jnp.broadcast_to(x[c : c + 1], (DH, DH)).T for c in range(rows)], axis=0
        )

    inverse = upright(inverse_rows)
    pull = upright(pull_rows)
    for h in range(heads):
        cols = slice(h * DH, (h + 1) * DH)
        out = out_ref[:, cols]
        gain_h = gain[:, cols]
        normed = (gain_h * out * inverse).astype(BF16)
        normed_ref[:, cols] = normed
        weighted = gain_h * (normed.astype(F32) - t_ref[:, cols].astype(F32))
        grad = (weighted * inverse - out * pull).astype(BF16)
        go_ref[:, cols] = grad
        put_state(1, h, contract(turned_ref[h], grad, NN))
    gather_states(1)

    def mix(h):
        mixing = contract(head(go_ref, h), head(v_ref, h), NT)
        mix_ref[h] = jnp.where(same_doc, mixing, 0.0).astype(BF16)

    def query_grad(h):
        far_part = contract(head(go_ref, h), take_state(0, h), NT)
        near = contract(mix_ref[h], head(k_ref, h), NN)
        gq_ref[:, h * DH : (h + 1) * DH] = (near + keep(use_in, far_part)).astype(BF16)

    def near_grads(h):
        return (
            contract(mix_ref[h], head(q_ref, h), TN),
            contract(attn_ref[h], head(go_ref, h), TN),
        )

    for h in range(heads):
        mix(h)
        query_grad(h)
    fold_column(1)
    hand_out(1)
    near = [near_grads(h) for h in range(heads)]
    for i in range(1, zs):
        sum_copy(i).wait_send()
    wait_slices(1, 1)
    for h in range(heads):
        suffix = take_state(1, h)
        cols = slice(h * DH, (h + 1) * DH)
        far_k = contract(head(v_ref, h), suffix, NT)
        far_v = contract(head(k_ref, h), suffix, NN)
        gk_ref[:, cols] = (near[h][0] + keep(use_out, far_k)).astype(BF16)
        gv_ref[:, cols] = (near[h][1] + keep(use_out, far_v)).astype(BF16)
    wait_sent(1, 1)


def flush(*refs):
    *arrays, sem = refs
    n = len(arrays) // 2
    copies = [pltpu.make_async_copy(arrays[i], arrays[n + i], sem.at[i]) for i in range(n)]
    for copy in copies:
        copy.start()
    for copy in copies:
        copy.wait()


def solution(mesh):
    seqs, zs = mesh.shape["seq"], mesh.shape["head"]

    def per_device(queries, key_feats, value_feats, targets, norm_gain, doc_lengths):
        tok, width = queries.shape
        ring = MAXDOC // tok
        heads = width // DH
        slices = width // ring
        states = pltpu.VMEM((2, ring, slices, DH), F32)
        vmem = pl.BlockSpec(memory_space=pltpu.VMEM)
        hbm = pl.BlockSpec(memory_space=pltpu.HBM)
        block = pltpu.VMEM((tok, width), BF16)
        held = (
            pl.pallas_call(
                functools.partial(kernel, seqs, ring, zs),
                out_shape=[pltpu.VMEM((tok, width), BF16)] * 4,
                in_specs=[hbm] * 6,
                out_specs=[vmem] * 4,
                scratch_shapes=[
                    pltpu.SMEM(doc_lengths.shape, jnp.int32),
                    block,
                    block,
                    block,
                    block,
                    pltpu.VMEM((1, width), F32),
                    pltpu.VMEM((2, ring, DH), F32),
                    pltpu.VMEM((2, ring, DH), F32),
                    states,
                    states,
                    states,
                    pltpu.VMEM((2, slices, DH), F32),
                    pltpu.VMEM((2, slices, DH), F32),
                    states,
                    states,
                    pltpu.VMEM((heads, DH, tok), BF16),
                    pltpu.VMEM((heads, tok, tok), BF16),
                    pltpu.VMEM((heads, tok, tok), BF16),
                    pltpu.VMEM((tok, width), F32),
                    pltpu.VMEM((tok, width), BF16),
                    pltpu.VMEM((3 * tok // DH, DH), F32),
                    pltpu.VMEM((zs, 3 * tok // DH, DH), F32),
                    pltpu.SemaphoreType.DMA((6,)),
                    pltpu.SemaphoreType.DMA((2, 2, ring)),
                    pltpu.SemaphoreType.DMA((2, 2, ring)),
                    pltpu.SemaphoreType.DMA((2, 2)),
                    pltpu.SemaphoreType.DMA((zs,)),
                    pltpu.SemaphoreType.DMA((zs,)),
                ],
                compiler_params=pltpu.CompilerParams(
                    collective_id=0, has_side_effects=True, vmem_limit_bytes=40 * 2**20
                ),
            )(
                *(
                    pltpu.with_memory_space_constraint(x, pltpu.HBM)
                    for x in (
                        doc_lengths,
                        queries,
                        key_feats,
                        value_feats,
                        targets,
                        norm_gain.reshape(1, width),
                    )
                )
            )
        )
        return tuple(
            pl.pallas_call(
                flush,
                out_shape=[jax.ShapeDtypeStruct((tok, width), BF16)] * 4,
                in_specs=[vmem] * 4,
                out_specs=[hbm] * 4,
                scratch_shapes=[pltpu.SemaphoreType.DMA((4,))],
                compiler_params=pltpu.CompilerParams(vmem_limit_bytes=8 * 2**20),
            )(*held)
        )

    spec = P("seq", "head")
    return jax.shard_map(
        per_device,
        mesh=mesh,
        in_specs=(spec, spec, spec, spec, P("head"), P()),
        out_specs=(spec, spec, spec, spec),
        check_vma=False,
    )
```
